32 devices in a mesh: dp: 8 (over z, x), shard: 4 (over y, core).
Axes of the slice: x: 2, y: 2, z: 4, core: 2. Of those that a mesh axis runs over, the one named last changes fastest.
Arguments:
- grads: bfloat16 [8, 384, 8192], P('dp', 'shard'), may hold values from -6 to 6
- momentum: float32 [8, 384, 8192], P('dp', 'shard'), may hold values from -6 to 6
- param: float32 [384, 8192], P('shard'), may hold values from -6 to 6
- thresholds: float32 [384], P('shard'), may hold values from 0.1 to 1
- sel_blocks: int32 [8, 4, 768], P(None, 'shard'), may hold values from 0 to 6143, as said below
- counts: int32 [8, 4], P(None, 'shard'), may hold values from 192 to 768, as said below
Outputs:
- new_momentum: float32 [8, 384, 8192], P('dp', 'shard')
- new_param: float32 [384, 8192], P('shard')
- compute_copy: bfloat16 [384, 8192], replicated
The draws below stay inside these ranges and needn't reach their ends.
Inputs may be any that keep to these rules, and one draw needn't show every extreme that they name: `sel_blocks`: within one replica and shard the 768 entries are distinct block numbers of that shard. `counts`: some replica has 768 live slots in every shard.
All inputs are finite; a program needn't handle non-finite values.
Results may differ from the reference program's by a relative error of at most 0.0019.
Values may be sent and summed in bfloat16 or wider, within the bound.
A program may use at most 128 MiB of HBM per device.

```python
import math
import jax
import jax.numpy as jnp
from jax import lax

D = 8192
NBLK = 6144
KMAX = 768
REPLICAS = 8
SHARDS = 4
ROWS = 384


def place_value(block_row, target, slot):
    current = block_row[slot]
    block_row = jnp.where(block_row == target, current, block_row)
    return block_row.at[slot].set(target)


def fix_row(block_row):
    return place_value(place_value(block_row, NBLK - 1, 0), 0, 1)


def shuffle_one(one_key):
    return jax.random.permutation(one_key, NBLK)


def selection(key):
    base_key = jax.random.fold_in(key, 17)
    perm_keys = jax.random.split(jax.random.fold_in(base_key, 1), REPLICAS * SHARDS)
    shuffled = jax.vmap(shuffle_one)(perm_keys).astype(jnp.int32).reshape(REPLICAS, SHARDS, NBLK)
    hot_replica = jax.random.randint(jax.random.fold_in(base_key, 2), (), 0, REPLICAS)
    fixed_rows = jax.vmap(jax.vmap(fix_row))(shuffled)
    is_hot = (jnp.arange(REPLICAS, dtype=jnp.int32) == hot_replica)[:, None, None]
    block_lists = jnp.where(is_hot, fixed_rows, shuffled)[:, :, :KMAX].astype(jnp.int32)
    live_counts = jax.random.randint(jax.random.fold_in(base_key, 3), (REPLICAS, SHARDS), max(KMAX // 4, 1), KMAX + 1)
    live_counts = jnp.where(is_hot[:, :, 0], KMAX, live_counts).astype(jnp.int32)
    return (block_lists, live_counts)


def draw_sel_blocks(key, part):
    return selection(key)[0]


def draw_counts(key, part):
    return selection(key)[1]


def block_scale(stream_key, shape, cuts, least, top_value):
    loudness = 1.0
    for dim, blocks in cuts:
        draws = jax.random.uniform(jax.random.fold_in(jax.random.fold_in(stream_key, 6), dim), (blocks,), jnp.float32, least / len(cuts), top_value / len(cuts))
        loudness = loudness * jnp.repeat(jnp.exp(draws), shape[dim] // blocks).reshape((-1,) + (1,) * (len(shape) - 1 - dim))
    return loudness


def scatter_about(own_key, shape, spread, bound, shards=(), kind=jnp.bfloat16):
    loudness = block_scale(own_key, shape, shards, -0.22, 0.18) if shards else 1.0
    array = jax.random.normal(own_key, shape, jnp.float32) * spread * loudness
    return jnp.minimum(jnp.maximum(array, -bound), bound).astype(kind)


def setup_inputs(seed: int = 0) -> dict:
    streams_of = jax.random.split(jax.random.key(seed), 7)
    return {
        "grads": scatter_about(streams_of[0], (REPLICAS, ROWS, D), 1.0, 6.0, ((0, 8), (1, 4))),
        "momentum": scatter_about(streams_of[1], (REPLICAS, ROWS, D), 1.0, 6.0, ((0, 8), (1, 4)), jnp.float32),
        "param": scatter_about(streams_of[2], (ROWS, D), 1.0, 6.0, ((0, 4),), jnp.float32),
        "thresholds": jnp.clip(jnp.exp(math.log(1.0) - 2.3025851 * jax.random.uniform(streams_of[3], (ROWS,), jnp.float32) ** block_scale(streams_of[3], (ROWS,), ((0, 4),), -0.2, 0.2)), 0.1, 1.0),
        "sel_blocks": draw_sel_blocks(jax.random.fold_in(streams_of[6], 71), 0),
        "counts": draw_counts(jax.random.fold_in(streams_of[6], 71), 0),
    }


beta_decay = 0.999
step_size = 0.1

def dct_table():
    positions = jnp.arange(128, dtype=jnp.int32)
    sample = (positions % 64)[:, None]
    freq = (positions % 64)[None, :]
    same_half = positions[:, None] // 64 == positions[None, :] // 64
    weights = jnp.where(freq == 0, math.sqrt(1.0 / 64.0), math.sqrt(2.0 / 64.0)).astype(jnp.float32)
    angles = ((2 * sample + 1) * freq).astype(jnp.float32) * (math.pi / 128.0)
    return jnp.where(same_half, weights * jnp.cos(angles), 0.0).astype(jnp.float32)

def reference(grads, momentum, param, thresholds, sel_blocks, counts):
    table = dct_table()
    per_row = D // 128
    thr_blocks = jnp.repeat(thresholds, per_row)[:, None]
    slot_index = jnp.arange(KMAX, dtype=jnp.int32)
    shard_base = (jnp.arange(SHARDS, dtype=jnp.int32) * NBLK)[:, None]

    def one_replica(total, inputs):
        grad_rep, mom_rep, sel_rep, count_rep = inputs
        blended = beta_decay * mom_rep + grad_rep.astype(jnp.float32)
        coefficients = jnp.dot(blended.reshape(-1, 128), table, precision=lax.Precision.HIGHEST, preferred_element_type=jnp.float32)
        shrunk = coefficients - jnp.clip(coefficients, -thr_blocks, thr_blocks)
        global_ids = (sel_rep + shard_base).reshape(-1).astype(jnp.int32)
        live_slots = (slot_index[None, :] < count_rep[:, None]).reshape(-1)
        chosen = jnp.where(live_slots[:, None], shrunk[global_ids], 0.0).astype(jnp.bfloat16)
        chosen = lax.optimization_barrier(chosen).astype(jnp.float32)
        sparse_dense = jnp.zeros_like(coefficients).at[global_ids].add(chosen)
        decoded = jnp.dot(sparse_dense, table.T, precision=lax.Precision.HIGHEST, preferred_element_type=jnp.float32)
        return (total + sparse_dense, blended - decoded.reshape(blended.shape))
    start_total = jnp.zeros((ROWS * per_row, 128), jnp.float32)
    total, new_momentum = lax.scan(one_replica, start_total, (grads, momentum, sel_blocks, counts))
    averaged = total / REPLICAS
    direction = jnp.dot(averaged, table.T, precision=lax.Precision.HIGHEST, preferred_element_type=jnp.float32).reshape(param.shape)
    update = jnp.tanh(direction * lax.rsqrt(lax.optimization_barrier(jnp.mean(direction * direction, axis=1, keepdims=True)) + 1e-06))
    new_param = param - step_size * update
    return (new_momentum, new_param, new_param.astype(jnp.bfloat16))
```

```python
import functools

import jax
import jax.numpy as jnp
import numpy as np
from jax import lax
from jax.experimental import pallas as pl
from jax.experimental.pallas import tpu as pltpu
from jax.sharding import PartitionSpec as P

BLK = 128
HALF = 64
beta_decay = 0.999
step_size = 0.1
UNROLL = 16
CLASSES = 4
PIECES = 16
PARTS = 4
CHUNKS = 6
QUAD = 4


def tables():
    pos = np.arange(BLK)
    sample, freq = (pos % HALF)[:, None], (pos % HALF)[None, :]
    same = pos[:, None] // HALF == pos[None, :] // HALF
    weights = np.where(freq == 0, np.sqrt(1.0 / HALF), np.sqrt(2.0 / HALF))
    table = np.where(same, weights * np.cos((2 * sample + 1) * freq * (np.pi / BLK)), 0.0).astype(np.float32)

    def wide(t):
        hi = t.astype(jnp.bfloat16)
        lo = (t - hi.astype(np.float32)).astype(jnp.bfloat16)
        half = np.concatenate([hi, lo], axis=1)
        return np.concatenate([half, half], axis=0)

    return wide(table), wide(table.T)


def split(x):
    hi = x.astype(jnp.bfloat16)
    lo = (x - hi.astype(jnp.float32)).astype(jnp.bfloat16)
    return jnp.concatenate([hi, lo], axis=1)


def both(x, w):
    y = jnp.dot(x, w, preferred_element_type=jnp.float32)
    return y[:, :BLK] + y[:, BLK:]


def tiles(x):
    return jnp.concatenate([x[:, c * BLK : (c + 1) * BLK] for c in range(x.shape[1] // BLK)], axis=0)


MESH = pl.DeviceIdType.MESH


def copy_to(src, dst, send, recv, peer):
    return pltpu.make_async_remote_copy(
        src_ref=src, dst_ref=dst, send_sem=send, recv_sem=recv, device_id=peer, device_id_type=MESH
    )


def step_kernel(
    reps, shards, mom, grad, param, thr_in, sel_in, counts_in, fwd_in, inv_in,
    newmom, newparam, rowsout,
    flat, total, scale, gbuf, buf, picked, thr, sel, place, counts, fwd, inv,
    send, recv, send2, recv2, local, loads,
):
    s = lax.axis_index("shard")
    me = lax.axis_index("dp")
    rows, D = total.shape
    slots = buf.shape[1]
    per_row = D // BLK
    deep_rows = rows // CHUNKS

    def fetch(src, dst, k):
        c = pltpu.make_async_copy(src, dst, local.at[k])
        c.start()
        return c

    def load(c, act):
        at = pl.ds(pl.multiple_of(c * deep_rows, 16), deep_rows)
        getattr(pltpu.make_async_copy(mom.at[at], newmom.at[at], loads.at[c, 0]), act)()
        getattr(pltpu.make_async_copy(grad.at[at], gbuf.at[at], loads.at[c, 1]), act)()

    where = fetch(sel_in.at[me], place, 0)
    limits = fetch(thr_in, thr, 1)
    amounts = fetch(counts_in, counts, 6)
    for c in range(CHUNKS):
        load(c, "start")
    tables_in = [fetch(fwd_in, fwd, 2), fetch(inv_in, inv, 3), fetch(sel_in, sel, 4)]
    owned = fetch(param, newparam, 5)

    group = shards // 2
    core, far = lax.rem(s, 2), s // 2
    flip1 = lambda v: v + 1 - 2 * lax.rem(v, 2)
    flip2 = lambda v: v + 2 - 4 * lax.rem(v // 2, 2)
    inner = {"shard": flip1(s)}
    outer = [2 * lax.rem(far + k, group) + core for k in range(1, group)]

    line, side = me // 2, lax.rem(me, 2)
    length = reps // 2
    up, down, across = {"dp": me + 2}, {"dp": me - 2}, {"dp": me + 1 - 2 * side}
    deep = {"dp": flip2(me)}
    has_up, has_down = line < length - 1, line > 0

    barrier = pltpu.get_barrier_semaphore()
    pl.semaphore_signal(barrier, inc=1, device_id=across, device_id_type=MESH)

    @pl.when(has_up)
    def _():
        pl.semaphore_signal(barrier, inc=1, device_id=up, device_id_type=MESH)

    @pl.when(has_down)
    def _():
        pl.semaphore_signal(barrier, inc=1, device_id=down, device_id_type=MESH)

    for peer in [inner] + [{"shard": o} for o in outer]:
        pl.semaphore_signal(barrier, inc=1, device_id=peer, device_id_type=MESH)

    def blend(c, carry):
        load(c, "wait")
        for r in range(deep_rows // 16):
            at = pl.ds(pl.multiple_of(c * deep_rows + 16 * r, 16), 16)
            base = (c * deep_rows + 16 * r) * per_row
            for k in range(per_row):
                lanes = pl.ds(k * BLK, BLK)
                x = beta_decay * newmom[at, lanes] + gbuf[at, lanes].astype(jnp.float32)
                for h in range(2):
                    flat[pl.ds(pl.multiple_of(base + h * 8 * per_row + k * 8, 8), 8), :] = x[h * 8 : h * 8 + 8]
        return carry

    lax.fori_loop(0, CHUNKS, blend, 0)
    where.wait()
    limits.wait()
    amounts.wait()
    for c in tables_in:
        c.wait()

    run = slots // PARTS
    shift = per_row.bit_length() - 1
    assert per_row == 1 << shift

    def pick_part(p):
        def pick(i, carry):
            base = p * run + i * UNROLL
            got = []
            for u in range(UNROLL):
                b = place[0, base + u]
                row = lax.shift_right_logical(b, shift)
                tile = (row & -8) * per_row + (b & (per_row - 1)) * 8
                got.append(flat[pl.ds(tile + (row & 7), 1), :])
            for u in range(UNROLL):
                picked[pl.ds(base + u, 1), :] = got[u]
            return carry

        lax.fori_loop(0, run // UNROLL, pick, 0)

    def encode_part(p):
        at = pl.ds(p * run, run)
        coef = both(split(picked[at, :]), fwd[...])
        ids = sel[me][:, p * run : (p + 1) * run]
        row = jnp.transpose(jnp.broadcast_to((ids // per_row).astype(jnp.float32), (BLK, run)))[:, :rows]
        lane = lax.broadcasted_iota(jnp.int32, (run, rows), 1).astype(jnp.float32)
        t = jnp.sum(jnp.where(row == lane, thr[...], 0.0), axis=1, keepdims=True)
        shrunk = coef - jnp.clip(coef, -t, t)
        live = lax.broadcasted_iota(jnp.int32, (run, BLK), 0) + p * run < counts[me]
        buf[me, at, :] = jnp.where(live, shrunk, 0.0).astype(jnp.bfloat16)

    def block(i, p, way, peer):
        ref = buf.at[i, pl.ds(p * run, run)]
        return copy_to(ref, ref, send.at[i, p, way], recv.at[i, p], peer)

    def first(p, act):
        @pl.when(has_up)
        def _():
            getattr(block(me, p, 0, up), act)()

        @pl.when(has_down)
        def _():
            getattr(block(me, p, 1, down), act)()

        getattr(block(me, p, 2, across), act)()

    half = PARTS // 2

    def relay(d, p, act):
        @pl.when(line >= d)
        def _():
            i = me - 2 * d
            if act == "start":
                block(i, p, 0, across).wait_recv()

            @pl.when(has_up)
            def _():
                getattr(block(i, p, 0, up), act)()

            @pl.when((p < half) | (line > d))
            def _():
                getattr(block(i, p, 2, across), act)()

        @pl.when(line + d < length)
        def _():
            i = me + 2 * d
            if act == "start":
                block(i, p, 1, across).wait_recv()

            @pl.when(has_down)
            def _():
                getattr(block(i, p, 1, down), act)()

            @pl.when((p < half) | (line + d < length - 1))
            def _():
                getattr(block(i, p, 2, across), act)()

    def dual(f, act):
        @pl.when(line == f)
        def _():
            i = 1 - side
            for p in range(half, PARTS):
                if act == "start":
                    block(i, p, 0, across).wait_recv()

                @pl.when(has_up)
                def _():
                    getattr(block(i, p, 0, up), act)()

        @pl.when(line + f == length - 1)
        def _():
            i = 2 * (length - 1) + 1 - side
            for p in range(half, PARTS):
                if act == "start":
                    block(i, p, 1, across).wait_recv()

                @pl.when(has_down)
                def _():
                    getattr(block(i, p, 1, down), act)()

    def spread(i, fresh=False):
        ids = sel[i]
        col = ids % per_row
        hot = ids // per_row == lax.broadcasted_iota(jnp.int32, (rows, slots), 0)
        rowhot = jnp.where(hot, 1.0, 0.0).astype(jnp.bfloat16)
        sub = jnp.transpose(jnp.broadcast_to((col % QUAD).astype(jnp.float32), (BLK, slots)))
        values = buf[i]
        rhs = jnp.concatenate(
            [values * jnp.where(sub == float(g), 1.0, 0.0).astype(jnp.bfloat16) for g in range(QUAD)], axis=1
        )
        quad = jnp.broadcast_to(col // QUAD, (16, slots))
        parts = []
        for u in range(per_row // QUAD):
            pick = jnp.where(quad == u, 1.0, 0.0).astype(jnp.bfloat16)
            parts.append(rowhot * jnp.concatenate([pick] * (rows // 16), axis=0))
        out = jnp.dot(jnp.concatenate(parts, axis=0), rhs, preferred_element_type=jnp.float32)
        for u in range(per_row // QUAD):
            at = pl.ds(u * (QUAD * BLK), QUAD * BLK)
            if fresh:
                total[:, at] = out[u * rows : (u + 1) * rows]
            else:
                total[:, at] += out[u * rows : (u + 1) * rows]

    for p in range(PARTS):
        pick_part(p)
        if p == 1:
            arrivals = 2 + len(outer) + jnp.where(has_up, 1, 0) + jnp.where(has_down, 1, 0)
            pl.semaphore_wait(barrier, arrivals)
        if p > 0:
            first(p - 1, "start")
        encode_part(p)

    spread_width = D // PIECES

    def feed(j, carry):
        at = pl.ds(pl.multiple_of(j * spread_width, BLK), spread_width)
        x = both(tiles(total[:, at]).astype(jnp.bfloat16), inv[:BLK, :])
        for c in range(spread_width // BLK):
            k = j * (spread_width // BLK) + c
            lanes = pl.ds(pl.multiple_of(k * BLK, BLK), BLK)
            for r in range(rows // 8):
                old = flat[pl.ds(pl.multiple_of((r * per_row + k) * 8, 8), 8), :]
                newmom[pl.ds(r * 8, 8), lanes] = old - x[c * rows + r * 8 : c * rows + r * 8 + 8]
        return carry

    spread(me, True)
    first(PARTS - 1, "start")
    lax.fori_loop(0, PIECES, feed, 0)
    relay(1, 0, "start")
    relay(1, 1, "start")
    dual(0, "start")

    def step(d, carry):
        for p in range(half, PARTS):
            relay(d, p, "start")

        def turn(t, carry):
            other = t // 2
            away = d - other
            at = line + (2 * lax.rem(t, 2) - 1) * away
            twin = (away == 0) & (lax.rem(t, 2) == 1)

            @pl.when(t == 2)
            def _():
                relay(d + 1, 0, "start")

            @pl.when(t == 3)
            def _():
                relay(d + 1, 1, "start")
                dual(d, "start")

            @pl.when((at >= 0) & (at < length) & jnp.logical_not(twin))
            def _():
                i = 2 * at + side + other * (1 - 2 * side)

                @pl.when(other == 1)
                def _():
                    ends = (at == 0) | (at == length - 1)
                    for p in range(half):
                        block(i, p, 2, across).wait_recv()

                    @pl.when(jnp.logical_not(ends))
                    def _():
                        for p in range(half, PARTS):
                            block(i, p, 2, across).wait_recv()

                spread(i)

            return carry

        lax.fori_loop(0, 4, turn, 0)
        return carry

    lax.fori_loop(1, length + 1, step, 0)

    def square(c, acc):
        a = total[:, pl.ds(pl.multiple_of(c * BLK, BLK), BLK)]
        return acc + a * a

    acc = lax.fori_loop(0, per_row, square, jnp.zeros((rows, BLK), jnp.float32), unroll=8)
    mean = jnp.sum(acc, axis=1, keepdims=True) * (1.0 / (D * reps * reps))
    scale[...] = jnp.broadcast_to(lax.rsqrt(mean + 1e-06) * (1.0 / reps), scale.shape)
    owned.wait()

    g = lax.rem(me, CLASSES)
    width = D // PIECES
    turns = PIECES // CLASSES

    def lanes(j):
        return pl.ds(pl.multiple_of(j * width, BLK), width)

    def piece(o, j, way, peer):
        ref = rowsout.at[o, :, lanes(j)]
        return copy_to(ref, ref, send2.at[o, j, way], recv2.at[o, j], peer)

    def own(j, k):
        return piece(s, j, k, {"shard": outer[k]})

    def compute(j):
        direction = both(split(tiles(total[:, lanes(j)])), inv[...])
        for c in range(width // BLK):
            at = pl.ds(pl.multiple_of(j * width + c * BLK, BLK), BLK)
            update = jnp.tanh(direction[c * rows : (c + 1) * rows] * scale[...])
            new = newparam[:, at] - step_size * update
            newparam[:, at] = new
            rowsout[s, :, at] = new.astype(jnp.bfloat16)

    def lead(k, carry):
        compute(g + CLASSES * k)

        @pl.when(k > 0)
        def _():
            for n in range(len(outer)):
                own(g + CLASSES * (k - 1), n).start()

        return carry

    def rest(turn):
        def one(k, carry):
            compute(lax.rem(g + turn, CLASSES) + CLASSES * k)
            return carry

        lax.fori_loop(0, turns, one, 0)

    sends = []

    def go(c):
        c.start()
        sends.append(c)

    lax.fori_loop(0, turns, lead, 0)
    rest(1)
    for n in range(len(outer)):
        own(g + CLASSES * (turns - 1), n).start()
        sends.extend(own(g + CLASSES * k, n) for k in range(turns))
    a, b, c = flip1(g), flip2(g), flip2(flip1(g))
    for k in range(turns):
        j = g + CLASSES * k
        for o in outer:
            piece(o, j, 0, inner).wait_recv()
            go(piece(o, j, 0, across))
            go(piece(o, j, 1, deep))
            go(piece(o, j, 2, inner))
        if k < 2:
            rest(k + 2)
        if k == 2:
            for direct in range(2, turns):
                for n in range(len(outer)):
                    go(own(c + CLASSES * direct, n))
    go(copy_to(rowsout.at[s], rowsout.at[s], send2.at[s, 0, group], recv2.at[s, PIECES], inner))
    for k in range(turns):
        for o in outer:
            j = a + CLASSES * k
            piece(o, j, 0, inner).wait_recv()
            if k == 0:
                go(piece(o, j, 1, deep))
            go(piece(o, j, 2, inner))
            j = b + CLASSES * k
            piece(o, j, 0, inner).wait_recv()
            if k == 1:
                go(piece(o, j, 0, across))
            go(piece(o, j, 2, inner))
    for k in range(turns):
        for o in outer:
            piece(o, c + CLASSES * k, 0, inner).wait_recv()
            go(piece(o, c + CLASSES * k, 2, inner))
    other = flip1(s)
    copy_to(rowsout.at[other], rowsout.at[other], send2.at[other, 0, 0], recv2.at[other, PIECES], inner).wait_recv()
    for o in outer:
        for j in range(PIECES):
            piece(flip1(o), j, 0, inner).wait_recv()
    for x in sends:
        x.wait_send()
    for p in range(PARTS):
        first(p, "wait_send")

    def drain(d, carry):
        for p in range(PARTS):
            relay(d, p, "wait_send")
        return carry

    lax.fori_loop(1, length, drain, 0)

    def undual(f, carry):
        dual(f, "wait_send")
        return carry

    lax.fori_loop(0, length, undual, 0)


def step(mom, grad, param, thr, sel, counts, fwd, inv, shards):
    reps, _, slots = sel.shape
    rows, D = param.shape
    vmem = pl.BlockSpec(memory_space=pltpu.VMEM)
    hbm = pl.BlockSpec(memory_space=pltpu.HBM)
    dma = pltpu.SemaphoreType.DMA
    return pl.pallas_call(
        functools.partial(step_kernel, reps, shards),
        out_shape=[
            pltpu.VMEM((rows, D), jnp.float32),
            pltpu.VMEM((rows, D), jnp.float32),
            pltpu.VMEM((shards, rows, D), jnp.bfloat16),
        ],
        in_specs=[hbm] * 8,
        out_specs=[vmem, vmem, vmem],
        scratch_shapes=[
            pltpu.VMEM((rows * (D // BLK), BLK), jnp.float32),
            pltpu.VMEM((rows, D), jnp.float32),
            pltpu.VMEM((rows, BLK), jnp.float32),
            pltpu.VMEM((rows, D), jnp.bfloat16),
            pltpu.VMEM((reps, slots, BLK), jnp.bfloat16),
            pltpu.VMEM((slots, BLK), jnp.float32),
            pltpu.VMEM(thr.shape, jnp.float32),
            pltpu.VMEM(sel.shape, jnp.int32),
            pltpu.SMEM((1, slots), jnp.int32),
            pltpu.SMEM(counts.shape, jnp.int32),
            pltpu.VMEM(fwd.shape, fwd.dtype),
            pltpu.VMEM(inv.shape, inv.dtype),
            dma((reps, PARTS, 3)),
            dma((reps, PARTS)),
            dma((shards, PIECES, max(3, shards))),
            dma((shards, PIECES + 1)),
            dma((7,)),
            dma((CHUNKS, 2)),
        ],
        compiler_params=pltpu.CompilerParams(
            collective_id=0, has_side_effects=True, vmem_limit_bytes=36 * 1024 * 1024
        ),
        name="step",
    )(*[pltpu.with_memory_space_constraint(x, pltpu.HBM) for x in (mom, grad, param, thr, sel, counts, fwd, inv)])


def place_kernel(n, *refs):
    sems = refs[-1]
    copies = []
    for i in range(n):
        c = pltpu.make_async_copy(refs[i], refs[n + i], sems.at[i])
        c.start()
        copies.append(c)
    for c in copies:
        c.wait()


def place(*arrays):
    n = len(arrays)
    return pl.pallas_call(
        functools.partial(place_kernel, n),
        out_shape=[jax.ShapeDtypeStruct(a.shape, a.dtype) for a in arrays],
        in_specs=[pl.BlockSpec(memory_space=pltpu.VMEM)] * n,
        out_specs=[pl.BlockSpec(memory_space=pl.ANY)] * n,
        scratch_shapes=[pltpu.SemaphoreType.DMA((n,))],
        compiler_params=pltpu.CompilerParams(vmem_limit_bytes=1024 * 1024),
        name="place",
    )(*[pltpu.with_memory_space_constraint(a, pltpu.VMEM) for a in arrays])


def on_device(grads, momentum, param, thresholds, sel_blocks, counts):
    rows, D = param.shape
    fwd, inv = (jnp.asarray(t) for t in tables())
    shards = lax.axis_size("shard")
    outs = step(
        momentum[0], grads[0], param, thresholds[None, :], sel_blocks, counts[:, 0], fwd, inv, shards
    )
    new_momentum, new_param, copies = place(*outs)
    return (new_momentum[None], new_param, copies.reshape(shards * rows, D))


def solution(mesh):
    placed = (
        P("dp", "shard", None),
        P("dp", "shard", None),
        P("shard", None),
        P("shard"),
        P(None, "shard", None),
        P(None, "shard"),
    )
    return jax.shard_map(
        on_device,
        mesh=mesh,
        in_specs=placed,
        out_specs=(P("dp", "shard", None), P("shard", None), P()),
        check_vma=False,
    )
```

```python
import functools

import jax
import jax.numpy as jnp
import numpy as np
from jax import lax
from jax.experimental import pallas as pl
from jax.experimental.pallas import tpu as pltpu
from jax.sharding import PartitionSpec as P

BLK = 128
HALF = 64
beta_decay = 0.999
step_size = 0.1
UNROLL = 48
CLASSES = 4
PIECES = 16
PARTS = 4
CHUNKS = 3
QUAD = 4
FEED = 16
LAG = 2


def tables():
    pos = np.arange(BLK)
    sample, freq = (pos % HALF)[:, None], (pos % HALF)[None, :]
    same = pos[:, None] // HALF == pos[None, :] // HALF
    weights = np.where(freq == 0, np.sqrt(1.0 / HALF), np.sqrt(2.0 / HALF))
    table = np.where(same, weights * np.cos((2 * sample + 1) * freq * (np.pi / BLK)), 0.0).astype(np.float32)

    def wide(t):
        hi = t.astype(jnp.bfloat16)
        lo = (t - hi.astype(np.float32)).astype(jnp.bfloat16)
        half = np.concatenate([hi, lo], axis=1)
        return np.concatenate([half, half], axis=0)

    return wide(table), wide(table.T)


def split(x):
    hi = x.astype(jnp.bfloat16)
    lo = (x - hi.astype(jnp.float32)).astype(jnp.bfloat16)
    return jnp.concatenate([hi, lo], axis=1)


def both(x, w):
    y = jnp.dot(x, w, preferred_element_type=jnp.float32)
    return y[:, :BLK] + y[:, BLK:]


def tiles(x):
    return jnp.concatenate([x[:, c * BLK : (c + 1) * BLK] for c in range(x.shape[1] // BLK)], axis=0)


MESH = pl.DeviceIdType.MESH


def copy_to(src, dst, send, recv, peer):
    return pltpu.make_async_remote_copy(
        src_ref=src, dst_ref=dst, send_sem=send, recv_sem=recv, device_id=peer, device_id_type=MESH
    )


def step_kernel(
    reps, shards, mom, grad, param, thr_in, sel_in, counts_in, fwd_in, inv_in,
    newmom, newparam, rowsout,
    flat, total, scale, gbuf, buf, picked, thr, sel, index, place, counts, fwd, inv,
    along, below, sides, duals, recv, owns, hops_x, hops_z, passes, recv_far, recv_near, whole, local, loads,
):
    s = lax.axis_index("shard")
    me = lax.axis_index("dp")
    rows, D = total.shape
    slots = buf.shape[1]
    per_row = D // BLK
    deep_rows = rows // CHUNKS

    def fetch(src, dst, k):
        c = pltpu.make_async_copy(src, dst, local.at[k])
        c.start()
        return c

    def load(c, act):
        at = pl.ds(pl.multiple_of(c * deep_rows, 16), deep_rows)
        getattr(pltpu.make_async_copy(mom.at[at], newmom.at[at], loads.at[c, 0]), act)()
        getattr(pltpu.make_async_copy(grad.at[at], gbuf.at[at], loads.at[c, 1]), act)()

    choices = fetch(sel_in, sel, 4)
    for c in range(CHUNKS):
        load(c, "start")
    small = [fetch(thr_in, thr, 1), fetch(counts_in, counts, 6), fetch(fwd_in, fwd, 2), fetch(inv_in, inv, 3)]

    group = shards // 2
    core, far = lax.rem(s, 2), s // 2
    flip1 = lambda v: v + 1 - 2 * lax.rem(v, 2)
    flip2 = lambda v: v + 2 - 4 * lax.rem(v // 2, 2)
    inner = {"shard": flip1(s)}
    outer = [2 * lax.rem(far + k, group) + core for k in range(1, group)]

    line, side = me // 2, lax.rem(me, 2)
    length = reps // 2
    up, down, across = {"dp": me + 2}, {"dp": me - 2}, {"dp": me + 1 - 2 * side}
    deep = {"dp": flip2(me)}
    has_up, has_down = line < length - 1, line > 0

    barrier = pltpu.get_barrier_semaphore()
    pl.semaphore_signal(barrier, inc=1, device_id=across, device_id_type=MESH)

    @pl.when(has_up)
    def _():
        pl.semaphore_signal(barrier, inc=1, device_id=up, device_id_type=MESH)

    @pl.when(has_down)
    def _():
        pl.semaphore_signal(barrier, inc=1, device_id=down, device_id_type=MESH)

    for peer in [inner] + [{"shard": o} for o in outer]:
        pl.semaphore_signal(barrier, inc=1, device_id=peer, device_id_type=MESH)

    def blend(c, carry):
        load(c, "wait")
        for r in range(deep_rows // 16):
            at = pl.ds(pl.multiple_of(c * deep_rows + 16 * r, 16), 16)
            base = (c * deep_rows + 16 * r) * per_row
            for k in range(per_row):
                lanes = pl.ds(k * BLK, BLK)
                x = beta_decay * newmom[at, lanes] + gbuf[at, lanes].astype(jnp.float32)
                for h in range(2):
                    flat[pl.ds(pl.multiple_of(base + h * 8 * per_row + k * 8, 8), 8), :] = x[h * 8 : h * 8 + 8]
        return carry

    choices.wait()
    ids = sel[me]
    row = ids // per_row
    index[...] = (row // 8) * (8 * per_row) + (ids % per_row) * 8 + row % 8
    blend(0, 0)
    where = fetch(index, place, 0)
    lax.fori_loop(1, CHUNKS, blend, 0)
    owned = fetch(param, newparam, 5)
    for c in small:
        c.wait()
    where.wait()
    run = slots // PARTS

    def pick_part(p):
        def pick(i, carry):
            base = p * run + i * UNROLL
            got = []
            for u in range(UNROLL):
                got.append(flat[pl.ds(place[0, base + u], 1), :])
            for u in range(UNROLL):
                picked[pl.ds(base + u, 1), :] = got[u]
            return carry

        lax.fori_loop(0, run // UNROLL, pick, 0)

    def encode_part(p):
        at = pl.ds(p * run, run)
        coef = both(split(picked[at, :]), fwd[...])
        ids = sel[me][:, p * run : (p + 1) * run]
        row = jnp.transpose(jnp.broadcast_to((ids // per_row).astype(jnp.float32), (BLK, run)))[:, :rows]
        lane = lax.broadcasted_iota(jnp.int32, (run, rows), 1).astype(jnp.float32)
        t = jnp.sum(jnp.where(row == lane, thr[...], 0.0), axis=1, keepdims=True)
        shrunk = coef - jnp.clip(coef, -t, t)
        live = lax.broadcasted_iota(jnp.int32, (run, BLK), 0) + p * run < counts[me]
        buf[me, at, :] = jnp.where(live, shrunk, 0.0).astype(jnp.bfloat16)

    half = PARTS // 2

    def block(i, p, sem, peer):
        ref = buf.at[i, pl.ds(p * run, run)]
        return copy_to(ref, ref, sem, recv.at[i, p], peer)

    def arrived(i, p):
        block(i, p, below.at[p], across).wait_recv()

    def first(p, act):
        @pl.when(has_up)
        def _():
            getattr(block(me, p, along.at[line, p], up), act)()

        @pl.when(has_down)
        def _():
            getattr(block(me, p, below.at[p], down), act)()

        getattr(block(me, p, sides.at[line, p], across), act)()

    def relay(d, p, act):
        @pl.when(line >= d)
        def _():
            i, at = me - 2 * d, line - d
            if act == "start":
                arrived(i, p)

            @pl.when(has_up)
            def _():
                getattr(block(i, p, along.at[at, p], up), act)()

            @pl.when((p < half) | (at > 0))
            def _():
                getattr(block(i, p, sides.at[at, p], across), act)()

        @pl.when(line + d < length)
        def _():
            i, at = me + 2 * d, line + d
            if act == "start":
                arrived(i, p)

            @pl.when(has_down)
            def _():
                getattr(block(i, p, along.at[at, p], down), act)()

            @pl.when((p < half) | (at < length - 1))
            def _():
                getattr(block(i, p, sides.at[at, p], across), act)()

    def dual(f, act):
        @pl.when(line == f)
        def _():
            i = 1 - side
            for p in range(half, PARTS):
                if act == "start":
                    arrived(i, p)

                @pl.when(has_up)
                def _():
                    getattr(block(i, p, duals.at[0, p - half], up), act)()

        @pl.when(line + f == length - 1)
        def _():
            i = 2 * (length - 1) + 1 - side
            for p in range(half, PARTS):
                if act == "start":
                    arrived(i, p)

                @pl.when(has_down)
                def _():
                    getattr(block(i, p, duals.at[1, p - half], down), act)()

    def spread(i, fresh=False):
        ids = sel[i]
        col = ids % per_row
        hot = ids // per_row == lax.broadcasted_iota(jnp.int32, (rows, slots), 0)
        rowhot = jnp.where(hot, 1.0, 0.0).astype(jnp.bfloat16)
        sub = jnp.transpose(jnp.broadcast_to((col % QUAD).astype(jnp.float32), (BLK, slots)))
        values = buf[i]
        rhs = jnp.concatenate(
            [values * jnp.where(sub == float(g), 1.0, 0.0).astype(jnp.bfloat16) for g in range(QUAD)], axis=1
        )
        quad = jnp.broadcast_to(col // QUAD, (16, slots))
        parts = []
        for u in range(per_row // QUAD):
            pick = jnp.where(quad == u, 1.0, 0.0).astype(jnp.bfloat16)
            parts.append(rowhot * jnp.concatenate([pick] * (rows // 16), axis=0))
        out = jnp.dot(jnp.concatenate(parts, axis=0), rhs, preferred_element_type=jnp.float32)
        for u in range(per_row // QUAD):
            at = pl.ds(u * (QUAD * BLK), QUAD * BLK)
            if fresh:
                total[:, at] = out[u * rows : (u + 1) * rows]
            else:
                total[:, at] += out[u * rows : (u + 1) * rows]

    for p in range(PARTS):
        pick_part(p)
        if p == 1:
            arrivals = 2 + len(outer) + jnp.where(has_up, 1, 0) + jnp.where(has_down, 1, 0)
            pl.semaphore_wait(barrier, arrivals)
        if p > 0:
            first(p - 1, "start")
        encode_part(p)

    spread_width = D // FEED

    def feed(j, carry):
        at = pl.ds(pl.multiple_of(j * spread_width, BLK), spread_width)
        x = both(tiles(total[:, at]).astype(jnp.bfloat16), inv[:BLK, :])
        for c in range(spread_width // BLK):
            k = j * (spread_width // BLK) + c
            lanes = pl.ds(pl.multiple_of(k * BLK, BLK), BLK)
            for r in range(rows // 8):
                old = flat[pl.ds(pl.multiple_of((r * per_row + k) * 8, 8), 8), :]
                newmom[pl.ds(r * 8, 8), lanes] = old - x[c * rows + r * 8 : c * rows + r * 8 + 8]
        return carry

    spread(me, True)
    first(PARTS - 1, "start")
    lax.fori_loop(0, FEED, feed, 0)
    relay(1, 0, "start")
    relay(1, 1, "start")
    dual(0, "start")

    def step(d, carry):
        for p in range(half, PARTS):
            relay(d, p, "start")

        def turn(t, carry):
            other = t // 2
            away = d - other
            at = line + (2 * lax.rem(t, 2) - 1) * away
            twin = (away == 0) & (lax.rem(t, 2) == 1)

            @pl.when(t == 2)
            def _():
                relay(d + 1, 0, "start")

            @pl.when(t == 3)
            def _():
                relay(d + 1, 1, "start")
                dual(d, "start")

            @pl.when((at >= 0) & (at < length) & jnp.logical_not(twin))
            def _():
                i = 2 * at + side + other * (1 - 2 * side)

                @pl.when(other == 1)
                def _():
                    ends = (at == 0) | (at == length - 1)
                    for p in range(half):
                        arrived(i, p)

                    @pl.when(jnp.logical_not(ends))
                    def _():
                        for p in range(half, PARTS):
                            arrived(i, p)

                spread(i)

            return carry

        lax.fori_loop(0, 4, turn, 0)
        return carry

    lax.fori_loop(1, length + 1, step, 0)

    def square(c, acc):
        a = total[:, pl.ds(pl.multiple_of(c * BLK, BLK), BLK)]
        return acc + a * a

    acc = lax.fori_loop(0, per_row, square, jnp.zeros((rows, BLK), jnp.float32), unroll=8)
    mean = jnp.sum(acc, axis=1, keepdims=True) * (1.0 / (D * reps * reps))
    scale[...] = jnp.broadcast_to(lax.rsqrt(mean + 1e-06) * (1.0 / reps), scale.shape)
    owned.wait()

    g = lax.rem(me, CLASSES)
    width = D // PIECES
    turns = PIECES // CLASSES

    def lanes(j):
        return pl.ds(pl.multiple_of(j * width, BLK), width)

    fan = range(len(outer))

    def piece(n, j, sem, peer):
        ref = rowsout.at[outer[n], :, lanes(j)]
        return copy_to(ref, ref, sem, recv_far.at[n, j], peer)

    def landed(n, j):
        piece(n, j, whole.at[0], inner).wait_recv()

    def beside(n, j):
        ref = rowsout.at[outer[n], :, lanes(j)]
        return copy_to(ref, ref, passes.at[n, j], recv_near.at[n, j], inner)

    def own(j, k, n):
        ref = rowsout.at[s, :, lanes(j)]
        return copy_to(ref, ref, owns.at[n, k], recv_far.at[group - 2 - n, j], {"shard": outer[n]})

    def compute(j):
        direction = both(split(tiles(total[:, lanes(j)])), inv[...])
        for c in range(width // BLK):
            at = pl.ds(pl.multiple_of(j * width + c * BLK, BLK), BLK)
            update = jnp.tanh(direction[c * rows : (c + 1) * rows] * scale[...])
            new = newparam[:, at] - step_size * update
            newparam[:, at] = new
            rowsout[s, :, at] = new.astype(jnp.bfloat16)

    a, b, c = flip1(g), flip2(g), flip2(flip1(g))
    quarter = turns // 4

    def lead(k, carry):
        compute(g + CLASSES * k)

        @pl.when(k > 0)
        def _():
            for n in fan:
                own(g + CLASSES * (k - 1), k - 1, n).start()

        return carry

    def follow(k, carry):
        compute(c + CLASSES * k)

        @pl.when(k == 0)
        def _():
            for n in fan:
                own(g + CLASSES * (turns - 1), turns - 1, n).start()

        @pl.when(k > 2 * quarter)
        def _():
            for n in fan:
                own(c + CLASSES * (k - 1), turns + k - 1 - 2 * quarter, n).start()

        return carry

    sends = []

    def go(c):
        c.start()
        sends.append(c)

    lax.fori_loop(0, turns, lead, 0)
    lax.fori_loop(0, turns, follow, 0)
    for n in fan:
        sends.extend(own(g + CLASSES * k, k, n) for k in range(turns))
        sends.extend(own(c + CLASSES * k, turns + k - 2 * quarter, n) for k in range(2 * quarter, turns - 1))

    def pass_on(k):
        for n in fan:
            j = a + CLASSES * k
            landed(n, j)
            if k < quarter:
                go(piece(n, j, hops_z.at[n, turns + k], deep))
            go(beside(n, j))
            j = b + CLASSES * k
            landed(n, j)
            if quarter <= k < 2 * quarter:
                go(piece(n, j, hops_x.at[n, turns + k - quarter], across))
            go(beside(n, j))

    for k in range(turns):
        j = g + CLASSES * k
        compute(a + CLASSES * k)
        for n in fan:
            landed(n, j)
            go(piece(n, j, hops_x.at[n, k], across))
            go(piece(n, j, hops_z.at[n, k], deep))
            go(beside(n, j))
        if k == 0:
            for n in fan:
                go(own(c + CLASSES * (turns - 1), 2 * turns - 1 - 2 * quarter, n))
        compute(b + CLASSES * k)
        if k >= LAG:
            pass_on(k - LAG)
    go(copy_to(rowsout.at[s], rowsout.at[s], whole.at[0], whole.at[1], inner))
    for k in range(turns - LAG, turns):
        pass_on(k)
    for k in range(turns):
        for n in fan:
            landed(n, c + CLASSES * k)
            go(beside(n, c + CLASSES * k))
    other = flip1(s)
    copy_to(rowsout.at[other], rowsout.at[other], whole.at[0], whole.at[1], inner).wait_recv()
    for n in fan:
        for j in range(PIECES):
            ref = rowsout.at[flip1(outer[n]), :, lanes(j)]
            copy_to(ref, ref, passes.at[n, j], recv_near.at[n, j], inner).wait_recv()
    for x in sends:
        x.wait_send()
    for p in range(PARTS):
        first(p, "wait_send")

    def drain(d, carry):
        for p in range(PARTS):
            relay(d, p, "wait_send")
        return carry

    lax.fori_loop(1, length, drain, 0)

    for p in range(half, PARTS):

        @pl.when(has_up)
        def _():
            block(1 - side, p, duals.at[0, p - half], up).wait_send()

        @pl.when(has_down)
        def _():
            block(2 * (length - 1) + 1 - side, p, duals.at[1, p - half], down).wait_send()


def step(mom, grad, param, thr, sel, counts, fwd, inv, shards):
    reps, _, slots = sel.shape
    rows, D = param.shape
    vmem = pl.BlockSpec(memory_space=pltpu.VMEM)
    hbm = pl.BlockSpec(memory_space=pltpu.HBM)
    dma = pltpu.SemaphoreType.DMA
    return pl.pallas_call(
        functools.partial(step_kernel, reps, shards),
        out_shape=[
            pltpu.VMEM((rows, D), jnp.float32),
            pltpu.VMEM((rows, D), jnp.float32),
            pltpu.VMEM((shards, rows, D), jnp.bfloat16),
        ],
        in_specs=[hbm] * 8,
        out_specs=[vmem, vmem, vmem],
        scratch_shapes=[
            pltpu.VMEM((rows * (D // BLK), BLK), jnp.float32),
            pltpu.VMEM((rows, D), jnp.float32),
            pltpu.VMEM((rows, BLK), jnp.float32),
            pltpu.VMEM((rows, D), jnp.bfloat16),
            pltpu.VMEM((reps, slots, BLK), jnp.bfloat16),
            pltpu.VMEM((slots, BLK), jnp.float32),
            pltpu.VMEM(thr.shape, jnp.float32),
            pltpu.VMEM(sel.shape, jnp.int32),
            pltpu.VMEM((1, slots), jnp.int32),
            pltpu.SMEM((1, slots), jnp.int32),
            pltpu.SMEM(counts.shape, jnp.int32),
            pltpu.VMEM(fwd.shape, fwd.dtype),
            pltpu.VMEM(inv.shape, inv.dtype),
            dma((reps // 2, PARTS)),
            dma((PARTS,)),
            dma((reps // 2, PARTS)),
            dma((2, PARTS // 2)),
            dma((reps, PARTS)),
            dma((shards // 2 - 1, 3 * PIECES // CLASSES // 2)),
            dma((shards // 2 - 1, 5 * PIECES // CLASSES // 4)),
            dma((shards // 2 - 1, 5 * PIECES // CLASSES // 4)),
            dma((shards // 2 - 1, PIECES)),
            dma((shards // 2 - 1, PIECES)),
            dma((shards // 2 - 1, PIECES)),
            dma((2,)),
            dma((7,)),
            dma((CHUNKS, 2)),
        ],
        compiler_params=pltpu.CompilerParams(
            collective_id=0, has_side_effects=True, vmem_limit_bytes=36 * 1024 * 1024
        ),
        name="step",
    )(*[pltpu.with_memory_space_constraint(x, pltpu.HBM) for x in (mom, grad, param, thr, sel, counts, fwd, inv)])


def place_kernel(n, *refs):
    sems = refs[-1]
    copies = []
    for i in range(n):
        c = pltpu.make_async_copy(refs[i], refs[n + i], sems.at[i])
        c.start()
        copies.append(c)
    for c in copies:
        c.wait()


def place(*arrays):
    n = len(arrays)
    return pl.pallas_call(
        functools.partial(place_kernel, n),
        out_shape=[jax.ShapeDtypeStruct(a.shape, a.dtype) for a in arrays],
        in_specs=[pl.BlockSpec(memory_space=pltpu.VMEM)] * n,
        out_specs=[pl.BlockSpec(memory_space=pl.ANY)] * n,
        scratch_shapes=[pltpu.SemaphoreType.DMA((n,))],
        compiler_params=pltpu.CompilerParams(vmem_limit_bytes=1024 * 1024),
        name="place",
    )(*[pltpu.with_memory_space_constraint(a, pltpu.VMEM) for a in arrays])


def on_device(grads, momentum, param, thresholds, sel_blocks, counts):
    rows, D = param.shape
    fwd, inv = (jnp.asarray(t) for t in tables())
    shards = lax.axis_size("shard")
    outs = step(
        momentum[0], grads[0], param, thresholds[None, :], sel_blocks, counts[:, 0], fwd, inv, shards
    )
    new_momentum, new_param, copies = place(*outs)
    return (new_momentum[None], new_param, copies.reshape(shards * rows, D))


def solution(mesh):
    placed = (
        P("dp", "shard", None),
        P("dp", "shard", None),
        P("shard", None),
        P("shard"),
        P(None, "shard", None),
        P(None, "shard"),
    )
    return jax.shard_map(
        on_device,
        mesh=mesh,
        in_specs=placed,
        out_specs=(P("dp", "shard", None), P("shard", None), P()),
        check_vma=False,
    )
```
